32 devices in a mesh: gx: 4 (over y, core), gy: 8 (over z, x).
Axes of the slice: x: 2, y: 2, z: 4, core: 2. Of those that a mesh axis runs over, the one named last changes fastest.
Arguments:
- hidden: bfloat16 [256, 8192], P('gx', 'gy'), may hold values from -12 to 12
- lengths: int32 [256], P('gy'), may hold values from 1 to 384
- draft_ids: int32 [256], P('gy'), may hold values from 0 to 31999
- attn_gain: bfloat16 [8192], P('gy'), may hold values from 0.099609375 to 1.8984375
- w_query: bfloat16 [8192, 8192], P('gy', 'gx'), may hold values from -0.0625 to 0.0625
- w_key: bfloat16 [8192, 1024], P('gy', 'gx'), may hold values from -0.0625 to 0.0625
- w_value: bfloat16 [8192, 1024], P('gy', 'gx'), may hold values from -0.0625 to 0.0625
- w_out: bfloat16 [8192, 8192], P('gx', 'gy'), may hold values from -0.0625 to 0.0625
- cache_k: bfloat16 [256, 8, 384, 128], P('gy', 'gx'), may hold values from -240 to 240
- cache_v: bfloat16 [256, 8, 384, 128], P('gy', 'gx'), may hold values from -6 to 6
- mlp_gain: bfloat16 [8192], P('gy'), may hold values from 0.099609375 to 1.8984375
- w_gate: bfloat16 [8192, 28672], P('gy', 'gx'), may hold values from -0.0625 to 0.0625
- w_up: bfloat16 [8192, 28672], P('gy', 'gx'), may hold values from -0.0625 to 0.0625
- w_down: bfloat16 [28672, 8192], P('gx', 'gy'), may hold values from -0.03125 to 0.03125
- final_gain: bfloat16 [8192], P('gy'), may hold values from 0.099609375 to 1.8984375
- w_head: bfloat16 [8192, 32000], P('gy', 'gx'), may hold values from -1 to 1
Outputs:
- log_probs: float32 [256, 32000], P('gy', 'gx')
- draft_logprob: float32 [256], P('gy')
The draws below stay inside these ranges and needn't reach their ends.
All inputs are finite; a program needn't handle non-finite values.
Results may differ from the reference program's by a relative error of at most 0.002.
Values may be sent and summed in bfloat16 or wider, within the bound.
No kernel may reach another device: no remote copies, remote signals or barrier semaphores. Data moves between devices by JAX's collectives and lax.ppermute only.
A program may use at most 192 MiB of HBM per device.

```python
import jax
import jax.numpy as jnp
from jax import lax

D = 8192
FF = 28672
VOCAB = 32000
HEADS = 64
KV_HEADS = 8
HEAD_DIM = 128
CTX = 384
BATCH = 256


def draw_hidden(key, part):
    sample = jnp.clip(jax.random.normal(jax.random.fold_in(key, 21), (BATCH, D), jnp.float32), -3.5, 3.5)
    ramp = jnp.arange(D, dtype=jnp.float32) / (D - 1)
    column_scale = jnp.exp(jnp.log(0.6) + (jnp.log(1.6) - jnp.log(0.6)) * ramp)
    sample = sample * column_scale[None, :]
    return sample.astype(jnp.bfloat16)


def draw_w_head(key, part):
    sample = jnp.clip(jax.random.normal(jax.random.fold_in(key, 31), (D, VOCAB), jnp.float32), -4.0, 4.0) * (3.0 * D ** (-0.5))
    return sample.astype(jnp.bfloat16)


def draw_cache_k(key, part):
    array_shape = (BATCH, KV_HEADS, CTX, HEAD_DIM)
    first_key = jax.random.fold_in(key, 11)
    sample = jnp.clip(jax.random.normal(first_key, array_shape, jnp.float32), -5.0, 5.0)
    return sample.astype(jnp.bfloat16)


def plant(drawn, rng, low, top_value):
    dims = drawn.shape
    index_at = [jax.random.randint(jax.random.fold_in(rng, axis), (), 0, dims[axis]) for axis in range(len(dims))]
    drawn = drawn.at[tuple(index_at)].set(low)
    longest = dims.index(max(dims))
    index_at[longest] = (index_at[longest] + 1) % dims[longest]
    return drawn.at[tuple(index_at)].set(top_value)


def level_of(key, extent, pieces, low, high):
    gain = 1.0
    for dim, blocks in pieces:
        heights = jax.random.uniform(jax.random.fold_in(jax.random.fold_in(key, 6), dim), (blocks,), jnp.float32, low / len(pieces), high / len(pieces))
        gain = gain * jnp.repeat(jnp.exp(heights), extent[dim] // blocks).reshape((-1,) + (1,) * (len(extent) - 1 - dim))
    return gain


def noise(key, shape, width, bound, shards=(), held_as=jnp.bfloat16):
    factor_of = level_of(key, shape, shards, -0.22, 0.18) if shards else 1.0
    values = jax.random.normal(key, shape, jnp.float32) * width * factor_of
    return jnp.minimum(jnp.maximum(values, -bound), bound).astype(held_as)


def setup_inputs(seed: int = 0) -> dict:
    streams_of = jax.random.split(jax.random.key(seed), 17)
    hidden = draw_hidden(jax.random.fold_in(streams_of[16], 71), 0)
    lengths = plant(jax.random.randint(streams_of[1], (BATCH,), 1, CTX + 1), jax.random.fold_in(streams_of[1], 1), 1, CTX).astype(jnp.int32)
    draft_ids = plant(jax.random.randint(streams_of[2], (BATCH,), 0, VOCAB), jax.random.fold_in(streams_of[2], 1), 0, VOCAB - 1).astype(jnp.int32)
    attn_gain = jnp.clip(1.0 + 0.18 * jax.random.normal(streams_of[3], (D,), jnp.float32), 0.099609375, 1.8984375).astype(jnp.bfloat16)
    w_query = noise(streams_of[4], (D, HEADS * HEAD_DIM), D ** -0.5, 0.0625, ((0, 8), (1, 4)))
    w_key = noise(streams_of[5], (D, KV_HEADS * HEAD_DIM), D ** -0.5, 0.0625, ((0, 8), (1, 4)))
    w_value = noise(streams_of[6], (D, KV_HEADS * HEAD_DIM), D ** -0.5, 0.0625, ((0, 8), (1, 4)))
    w_out = noise(streams_of[7], (HEADS * HEAD_DIM, D), (HEADS * HEAD_DIM) ** -0.5, 0.0625, ((0, 4), (1, 8)))
    cache_k = draw_cache_k(jax.random.fold_in(streams_of[16], 71), 0)
    cache_v = noise(streams_of[9], (BATCH, KV_HEADS, CTX, HEAD_DIM), 1.0, 6.0, ((0, 8), (1, 4)))
    mlp_gain = jnp.clip(1.0 + 0.18 * jax.random.normal(streams_of[10], (D,), jnp.float32), 0.099609375, 1.8984375).astype(jnp.bfloat16)
    w_gate = noise(streams_of[11], (D, FF), D ** -0.5, 0.0625, ((0, 8), (1, 4)))
    w_up = noise(streams_of[12], (D, FF), D ** -0.5, 0.0625, ((0, 8), (1, 4)))
    w_down = noise(streams_of[13], (FF, D), FF ** -0.5, 0.03125, ((0, 4), (1, 8)))
    final_gain = jnp.clip(1.0 + 0.18 * jax.random.normal(streams_of[14], (D,), jnp.float32), 0.099609375, 1.8984375).astype(jnp.bfloat16)
    w_head = draw_w_head(jax.random.fold_in(streams_of[16], 71), 0)
    return dict(hidden=hidden, lengths=lengths, draft_ids=draft_ids, attn_gain=attn_gain, w_query=w_query, w_key=w_key, w_value=w_value, w_out=w_out, cache_k=cache_k, cache_v=cache_v, mlp_gain=mlp_gain, w_gate=w_gate, w_up=w_up, w_down=w_down, final_gain=final_gain, w_head=w_head)


epsilon = 1e-05

def rotate(vectors, position):
    half_dim = vectors.shape[-1] // 2
    frequency = jnp.exp(-jnp.log(10000.0) * jnp.arange(half_dim, dtype=jnp.float32) * (2.0 / vectors.shape[-1]))
    angle_table = position[:, None, None] * frequency
    cosine = jnp.cos(angle_table)
    sine_part = jnp.sin(angle_table)
    first_half = vectors[..., :half_dim]
    second_half = vectors[..., half_dim:]
    return jnp.concatenate([first_half * cosine - second_half * sine_part, second_half * cosine + first_half * sine_part], axis=-1)

def normalize(activity, gain_row):
    squares = lax.optimization_barrier(jnp.sum(activity * activity, axis=1))
    factor = lax.rsqrt(squares / D + epsilon)
    return (activity * factor[:, None] * gain_row.astype(jnp.float32)).astype(jnp.bfloat16)

def attend_one(packed):
    queries, own_key, own_value, cached_keys, values, usable = packed
    scaling = queries.shape[-1] ** (-0.5)
    queries = queries.astype(jnp.float32)
    scores = jnp.einsum('bgd,btd->bgt', queries, cached_keys.astype(jnp.float32)) * scaling
    own_score = jnp.einsum('bgd,bd->bg', queries, own_key.astype(jnp.float32)) * scaling
    scores = jnp.where(usable[:, None, :], scores, -jnp.inf)
    highest = jnp.maximum(lax.optimization_barrier(jnp.max(scores, axis=2)), own_score)
    weights = jnp.exp(scores - highest[:, :, None])
    own_weight = jnp.exp(own_score - highest)
    denominator = lax.optimization_barrier(jnp.sum(weights, axis=2)) + own_weight
    weights = (weights / denominator[:, :, None]).astype(jnp.bfloat16)
    own_weight = (own_weight / denominator).astype(jnp.bfloat16)
    blended = jnp.einsum('bgt,btd->bgd', weights.astype(jnp.float32), values.astype(jnp.float32))
    blended = blended + own_weight.astype(jnp.float32)[:, :, None] * own_value.astype(jnp.float32)[:, None, :]
    return blended.astype(jnp.bfloat16)

def reference(hidden, lengths, draft_ids, attn_gain, w_query, w_key, w_value, w_out, cache_k, cache_v, mlp_gain, w_gate, w_up, w_down, final_gain, w_head):
    residual = hidden.astype(jnp.float32)
    tokens = normalize(residual, attn_gain)
    position = lengths.astype(jnp.float32)
    query_raw = jnp.dot(tokens, w_query, preferred_element_type=jnp.float32)
    key_raw = jnp.dot(tokens, w_key, preferred_element_type=jnp.float32)
    value_raw = jnp.dot(tokens, w_value, preferred_element_type=jnp.float32)
    queries = rotate(query_raw.reshape(BATCH, HEADS, HEAD_DIM), position).astype(jnp.bfloat16)
    new_keys = rotate(key_raw.reshape(BATCH, KV_HEADS, HEAD_DIM), position).astype(jnp.bfloat16)
    new_values = value_raw.reshape(BATCH, KV_HEADS, HEAD_DIM).astype(jnp.bfloat16)
    queries = queries.reshape(BATCH, KV_HEADS, HEADS // KV_HEADS, HEAD_DIM)
    usable = jnp.arange(CTX, dtype=jnp.int32)[None, :] < lengths[:, None]
    usable_all = jnp.broadcast_to(usable[None], (KV_HEADS, BATCH, CTX))
    attended = lax.map(attend_one, (jnp.moveaxis(queries, 1, 0), jnp.moveaxis(new_keys, 1, 0), jnp.moveaxis(new_values, 1, 0), jnp.moveaxis(cache_k, 1, 0), jnp.moveaxis(cache_v, 1, 0), usable_all))
    attended = jnp.moveaxis(attended, 0, 1).reshape(BATCH, HEADS * HEAD_DIM)
    after_attention = (residual + jnp.dot(attended, w_out, preferred_element_type=jnp.float32)).astype(jnp.bfloat16)
    mlp_tokens = normalize(after_attention.astype(jnp.float32), mlp_gain)
    gate_sum = jnp.dot(mlp_tokens, w_gate, preferred_element_type=jnp.float32)
    up_sum = jnp.dot(mlp_tokens, w_up, preferred_element_type=jnp.float32)
    activation = (jax.nn.silu(gate_sum) * up_sum).astype(jnp.bfloat16)
    after_mlp = (after_attention.astype(jnp.float32) + jnp.dot(activation, w_down, preferred_element_type=jnp.float32)).astype(jnp.bfloat16)
    final_tokens = normalize(after_mlp.astype(jnp.float32), final_gain)
    logits = jnp.dot(final_tokens, w_head, preferred_element_type=jnp.float32)
    log_probs = logits - jax.nn.logsumexp(logits, axis=1, keepdims=True)
    draft_logprob = jnp.take_along_axis(log_probs, draft_ids[:, None].astype(jnp.int32), axis=1)[:, 0]
    return (log_probs, draft_logprob)
```

```python
import jax
import jax.numpy as jnp
from jax import lax
from jax.sharding import PartitionSpec as P

HEAD_DIM = 128
epsilon = 1e-05
f32, bf16 = jnp.float32, jnp.bfloat16


def factor_axis(size):
    minor = 1
    while (2 * minor) ** 2 <= size:
        minor *= 2
    return size // minor, minor


def swap(x, axis, mask):
    return lax.ppermute(x, axis, [(i, i ^ mask) for i in range(lax.axis_size(axis))])


def pick(x, index, dim=0):
    return lax.dynamic_index_in_dim(x, index, dim, keepdims=False)


def mm(a, b):
    return jnp.dot(a, b, preferred_element_type=f32)


def sum_all(x, axis):
    mask = 1
    while mask < lax.axis_size(axis):
        x = x + swap(x, axis, mask)
        mask *= 2
    return x


def scatter_rows(partial, axis):
    major, minor = factor_axis(lax.axis_size(axis))
    me = lax.axis_index(axis)
    hi, lo = me // minor, me % minor
    rows, width = partial.shape
    blocks = partial.reshape(major, minor, rows // (major * minor), width)
    kept = pick(blocks, lo, 1)
    for k in range(1, minor):
        kept = kept + swap(pick(blocks, lo ^ k, 1).astype(bf16), axis, k).astype(f32)
    own = pick(kept, hi)
    for k in range(1, major):
        own = own + swap(pick(kept, hi ^ k).astype(bf16), axis, k * minor).astype(f32)
    return own


def gather_blocks(own, axis):
    major, minor = factor_axis(lax.axis_size(axis))
    me = lax.axis_index(axis)
    out = []
    for k in range(major):
        part = swap(own, axis, k * minor) if k else own
        out.append((me ^ (k * minor), part))
        for j in range(1, minor):
            out.append((me ^ (k * minor + j), swap(part, axis, j)))
    return out


def gather_rows(own, axis):
    rows, width = own.shape
    whole = jnp.zeros((lax.axis_size(axis), rows, width), own.dtype)
    for index, block in gather_blocks(own, axis):
        whole = lax.dynamic_update_index_in_dim(whole, block, index, 0)
    return whole.reshape(-1, width)


def add_over(partial, residual, axis):
    major, minor = factor_axis(lax.axis_size(axis))
    lo = lax.axis_index(axis) % minor
    rows, width = partial.shape
    blocks = partial.reshape(minor, rows // minor, width)
    kept = pick(blocks, lo)
    for k in range(1, minor):
        kept = kept + swap(pick(blocks, lo ^ k).astype(bf16), axis, k).astype(f32)
    total = kept
    mine = kept.astype(bf16)
    for k in range(1, major):
        total = total + swap(mine, axis, k * minor).astype(f32)
    total = (total + pick(residual.reshape(blocks.shape), lo).astype(f32)).astype(bf16)
    whole = jnp.zeros(blocks.shape, bf16)
    whole = lax.dynamic_update_index_in_dim(whole, total, lo, 0)
    for k in range(1, minor):
        whole = lax.dynamic_update_index_in_dim(whole, swap(total, axis, k), lo ^ k, 0)
    return whole.reshape(rows, width)


def factor_of(x, width):
    x = x.astype(f32)
    return lax.rsqrt(sum_all(jnp.sum(x * x, axis=1), "gy") / width + epsilon)


def scaled(x, gain):
    return (x.astype(f32) * gain.astype(f32)).astype(bf16)


def rotate(vectors, position):
    half = vectors.shape[-1] // 2
    frequency = jnp.exp(
        -jnp.log(10000.0) * jnp.arange(half, dtype=f32) * (2.0 / vectors.shape[-1])
    )
    angle = position[:, None, None] * frequency
    cosine, sine = jnp.cos(angle), jnp.sin(angle)
    first, second = vectors[..., :half], vectors[..., half:]
    return jnp.concatenate(
        [first * cosine - second * sine, second * cosine + first * sine], axis=-1
    )


def attend_one(queries, own_key, own_value, keys, values, usable):
    scaling = queries.shape[-1] ** (-0.5)
    scores = jnp.einsum("bgd,btd->bgt", queries, keys, preferred_element_type=f32) * scaling
    own_score = jnp.einsum("bgd,bd->bg", queries, own_key, preferred_element_type=f32) * scaling
    scores = jnp.where(usable[:, None, :], scores, -jnp.inf)
    highest = jnp.maximum(jnp.max(scores, axis=2), own_score)
    weights = jnp.exp(scores - highest[:, :, None])
    own_weight = jnp.exp(own_score - highest)
    denominator = jnp.sum(weights, axis=2) + own_weight
    weights = (weights / denominator[:, :, None]).astype(bf16)
    own_weight = (own_weight / denominator).astype(bf16)
    blended = jnp.einsum("bgt,btd->bgd", weights, values, preferred_element_type=f32)
    blended = blended + own_weight.astype(f32)[:, :, None] * own_value.astype(f32)[:, None, :]
    return blended.astype(bf16)


def shards(
    hidden, lengths, draft_ids, attn_gain, w_query, w_key, w_value, w_out, cache_k, cache_v,
    mlp_gain, w_gate, w_up, w_down, final_gain, w_head,
):
    gy = lax.axis_size("gy")
    me = lax.axis_index("gy")
    width = hidden.shape[1] * gy
    local = lengths.shape[0]
    major, minor = factor_axis(gy)

    residual = lax.all_gather(hidden, "gx", axis=0, tiled=True)
    tokens = scaled(residual, attn_gain)
    factor = factor_of(residual, width)
    own_factor = pick(factor.reshape(gy, local), me)
    projected = scatter_rows(
        jnp.concatenate([mm(tokens, w_query), mm(tokens, w_key), mm(tokens, w_value)], axis=1), "gy"
    )
    projected = projected * own_factor[:, None]
    query_width, key_width = w_query.shape[1], w_key.shape[1]
    position = lengths.astype(f32)
    heads = lambda a: a.reshape(local, -1, HEAD_DIM)
    queries = rotate(heads(projected[:, :query_width]), position).astype(bf16)
    new_keys = rotate(heads(projected[:, query_width : query_width + key_width]), position).astype(bf16)
    new_values = heads(projected[:, query_width + key_width :]).astype(bf16)
    queries = queries.reshape(local, new_keys.shape[1], -1, HEAD_DIM)
    usable = jnp.arange(cache_k.shape[2], dtype=jnp.int32)[None, :] < lengths[:, None]
    attended = jax.vmap(attend_one, in_axes=(1, 1, 1, 1, 1, None), out_axes=1)(
        queries, new_keys, new_values, cache_k, cache_v, usable
    ).reshape(local, query_width)

    all_heads = gather_rows(attended, "gy")
    after_attention = add_over(mm(all_heads, w_out), residual, "gx")

    tokens = scaled(after_attention, mlp_gain)
    factor = factor_of(after_attention, width)
    block = w_gate.shape[1] // gy

    def gate_up(index):
        cut = lambda w: lax.dynamic_slice_in_dim(w, index * block, block, 1)
        return jnp.concatenate([mm(tokens, cut(w_gate)), mm(tokens, cut(w_up))], axis=1)

    arrived = {}
    for k in reversed(range(major)):
        arrived[k] = [
            swap(gate_up(me ^ (k * minor + j)).astype(bf16), "gy", j) for j in range(1, minor)
        ]
    total = None
    sent = []
    for k in reversed(range(major)):
        total = gate_up(me ^ (k * minor))
        for part in arrived[k]:
            total = total + part.astype(f32)
        if k:
            sent.append(swap(total.astype(bf16), "gy", k * minor))
    for part in sent:
        total = total + part.astype(f32)
    total = total * factor[:, None]
    activation = (jax.nn.silu(total[:, :block]) * total[:, block:]).astype(bf16)
    down = 0.0
    for index, part in gather_blocks(activation, "gy"):
        down = down + mm(part, lax.dynamic_slice_in_dim(w_down, index * block, block, 0))
    after_mlp = add_over(down, after_attention, "gx")

    tokens = scaled(after_mlp, final_gain)
    factor = factor_of(after_mlp, width)
    own_factor = pick(factor.reshape(gy, local), me)
    vocab = w_head.shape[1]
    step = 2048
    pieces = []
    for start in range(0, vocab, step):
        pieces.append(scatter_rows(mm(tokens, w_head[:, start : start + step]), "gy") * own_factor[:, None])
    first = lax.axis_index("gx") * vocab
    tops, sums, picked = [], [], 0.0
    for start, piece in zip(range(0, vocab, step), pieces, strict=True):
        ids = jnp.arange(piece.shape[1], dtype=jnp.int32)[None, :] + (first + start)
        picked = picked + jnp.sum(jnp.where(ids == draft_ids[:, None], piece, 0.0), axis=1)
        top = jnp.max(piece, axis=1)
        tops.append(top)
        sums.append(jnp.sum(jnp.exp(piece - top[:, None]), axis=1))
    top = jnp.max(jnp.stack(tops), axis=0)
    total = sum(s * jnp.exp(t - top) for s, t in zip(sums, tops, strict=True))
    stats = jnp.stack([top, total, picked])
    mask = 1
    while mask < lax.axis_size("gx"):
        other = swap(stats, "gx", mask)
        high = jnp.maximum(stats[0], other[0])
        stats = jnp.stack(
            [
                high,
                stats[1] * jnp.exp(stats[0] - high) + other[1] * jnp.exp(other[0] - high),
                stats[2] + other[2],
            ]
        )
        mask *= 2
    normalizer = stats[0] + jnp.log(stats[1])
    return (jnp.concatenate(pieces, axis=1) - normalizer[:, None], stats[2] - normalizer)


def solution(mesh):
    return jax.shard_map(
        shards,
        mesh=mesh,
        in_specs=(
            P("gx", "gy"), P("gy"), P("gy"), P("gy"), P("gy", "gx"), P("gy", "gx"), P("gy", "gx"),
            P("gx", "gy"), P("gy", "gx", None, None), P("gy", "gx", None, None), P("gy"),
            P("gy", "gx"), P("gy", "gx"), P("gx", "gy"), P("gy"), P("gy", "gx"),
        ),
        out_specs=(P("gy", "gx"), P("gy")),
        check_vma=False,
    )
```

```python
import jax
import jax.numpy as jnp
from jax import lax
from jax.sharding import PartitionSpec as P


HEAD_DIM = 128
epsilon = 1e-05
HEAD_PARTS = (0.28, 0.27, 0.22, 0.14)
f32, bf16 = jnp.float32, jnp.bfloat16


def factor_axis(size):
    minor = 1
    while (2 * minor) ** 2 <= size:
        minor *= 2
    return size // minor, minor


def swap(x, axis, mask):
    return lax.ppermute(x, axis, [(i, i ^ mask) for i in range(lax.axis_size(axis))])


def pick(x, index, dim=0):
    return lax.dynamic_index_in_dim(x, index, dim, keepdims=False)


def mm(a, b):
    return jnp.dot(a, b, preferred_element_type=f32)


def sum_all(x, axis):
    mask = 1
    while mask < lax.axis_size(axis):
        x = x + swap(x, axis, mask)
        mask *= 2
    return x


def scatter_rows(partial, axis):
    major, minor = factor_axis(lax.axis_size(axis))
    me = lax.axis_index(axis)
    hi, lo = me // minor, me % minor
    rows, width = partial.shape
    blocks = partial.reshape(major, minor, rows // (major * minor), width)
    kept = pick(blocks, lo, 1)
    for k in range(1, minor):
        kept = kept + swap(pick(blocks, lo ^ k, 1).astype(bf16), axis, k).astype(f32)
    mask = 1
    while mask < major:
        bit = (hi // mask) % 2
        pairs = kept.reshape(-1, 2, *kept.shape[1:])
        kept = pick(pairs, bit, 1) + swap(
            pick(pairs, 1 - bit, 1).astype(bf16), axis, mask * minor
        ).astype(f32)
        mask *= 2
    return kept.reshape(-1, width)


def gather_blocks(own, axis, me=None):
    major, minor = factor_axis(lax.axis_size(axis))
    me = lax.axis_index(axis) if me is None else me
    parts = {0: own}
    bit = major // 2
    while bit:
        for k in list(parts):
            parts[k ^ bit] = swap(parts[k], axis, bit * minor)
        bit //= 2
    out = []
    for k, part in parts.items():
        out.append((me ^ (k * minor), part))
        for j in range(1, minor):
            out.append((me ^ (k * minor + j), swap(part, axis, j)))
    return out


def gather_rows(own, axis):
    rows, width = own.shape
    whole = jnp.zeros((lax.axis_size(axis), rows, width), own.dtype)
    for index, block in gather_blocks(own, axis):
        whole = lax.dynamic_update_index_in_dim(whole, block, index, 0)
    return whole.reshape(-1, width)


def add_over(partial, residual, axis):
    major, minor = factor_axis(lax.axis_size(axis))
    lo = lax.axis_index(axis) % minor
    rows, width = partial.shape
    blocks = partial.reshape(minor, rows // minor, width)
    kept = pick(blocks, lo)
    for k in range(1, minor):
        kept = kept + swap(pick(blocks, lo ^ k).astype(bf16), axis, k).astype(f32)
    total = kept
    mine = kept.astype(bf16)
    for k in range(1, major):
        total = total + swap(mine, axis, k * minor).astype(f32)
    total = (total + pick(residual.reshape(blocks.shape), lo).astype(f32)).astype(bf16)
    whole = jnp.zeros(blocks.shape, bf16)
    whole = lax.dynamic_update_index_in_dim(whole, total, lo, 0)
    for k in range(1, minor):
        whole = lax.dynamic_update_index_in_dim(whole, swap(total, axis, k), lo ^ k, 0)
    return whole.reshape(rows, width)


def factor_of(x, width):
    x = x.astype(f32)
    return lax.rsqrt(sum_all(jnp.sum(x * x, axis=1), "gy") / width + epsilon)


def scaled(x, gain):
    return (x.astype(f32) * gain.astype(f32)).astype(bf16)


def rotate(vectors, position):
    half = vectors.shape[-1] // 2
    frequency = jnp.exp(
        -jnp.log(10000.0) * jnp.arange(half, dtype=f32) * (2.0 / vectors.shape[-1])
    )
    angle = position[:, None, None] * frequency
    cosine, sine = jnp.cos(angle), jnp.sin(angle)
    first, second = vectors[..., :half], vectors[..., half:]
    return jnp.concatenate(
        [first * cosine - second * sine, second * cosine + first * sine], axis=-1
    )


def attend_one(queries, own_key, own_value, keys, values, usable):
    scaling = queries.shape[-1] ** (-0.5)
    scores = jnp.einsum("bgd,btd->bgt", queries, keys, preferred_element_type=f32) * scaling
    own_score = jnp.einsum("bgd,bd->bg", queries, own_key, preferred_element_type=f32) * scaling
    scores = jnp.where(usable[:, None, :], scores, -jnp.inf)
    highest = jnp.maximum(jnp.max(scores, axis=2), own_score)
    weights = jnp.exp(scores - highest[:, :, None])
    own_weight = jnp.exp(own_score - highest)
    denominator = jnp.sum(weights, axis=2) + own_weight
    weights = (weights / denominator[:, :, None]).astype(bf16)
    own_weight = (own_weight / denominator).astype(bf16)
    blended = jnp.einsum("bgt,btd->bgd", weights, values, preferred_element_type=f32)
    blended = blended + own_weight.astype(f32)[:, :, None] * own_value.astype(f32)[:, None, :]
    return blended.astype(bf16)


def head_starts(vocab):
    cuts = [0]
    for part in HEAD_PARTS:
        cuts.append(min(vocab, cuts[-1] + max(1, round(vocab * part / 128)) * 128))
    return cuts + [vocab]


def shards(
    hidden, lengths, draft_ids, attn_gain, w_query, w_key, w_value, w_out, cache_k, cache_v,
    mlp_gain, w_gate, w_up, w_down, final_gain, w_head,
):
    gy = lax.axis_size("gy")
    me = lax.axis_index("gy")
    width = hidden.shape[1] * gy
    local = lengths.shape[0]
    major, minor = factor_axis(gy)

    residual = lax.all_gather(hidden, "gx", axis=0, tiled=True)
    tokens = scaled(residual, attn_gain)
    factor = factor_of(residual, width)
    own_factor = pick(factor.reshape(gy, local), me)
    products = [mm(tokens, w) for w in (w_query, w_key, w_value)]
    projected = scatter_rows(jnp.concatenate(products, axis=1), "gy")
    projected = projected * own_factor[:, None]
    query_width, key_width = w_query.shape[1], w_key.shape[1]
    position = lengths.astype(f32)
    heads = lambda a: a.reshape(local, -1, HEAD_DIM)
    queries = rotate(heads(projected[:, :query_width]), position).astype(bf16)
    new_keys = rotate(heads(projected[:, query_width : query_width + key_width]), position).astype(bf16)
    new_values = heads(projected[:, query_width + key_width :]).astype(bf16)
    queries = queries.reshape(local, new_keys.shape[1], -1, HEAD_DIM)
    usable = jnp.arange(cache_k.shape[2], dtype=jnp.int32)[None, :] < lengths[:, None]
    attended = jax.vmap(attend_one, in_axes=(1, 1, 1, 1, 1, None), out_axes=1)(
        queries, new_keys, new_values, cache_k, cache_v, usable
    ).reshape(local, query_width)

    all_heads = gather_rows(attended, "gy")
    after_attention = add_over(mm(all_heads, w_out), residual, "gx")

    tokens = scaled(after_attention, mlp_gain)
    factor = factor_of(after_attention, width)
    block = w_gate.shape[1] // gy

    def gate_up(index):
        cut = lambda w: lax.dynamic_slice_in_dim(w, index * block, block, 1)
        return jnp.concatenate([mm(tokens, cut(w_gate)), mm(tokens, cut(w_up))], axis=1)

    subs = cuts(block)
    turns = visits(major)
    sends, arrived = {}, {}
    for k in turns:
        for j in range(1, minor):
            sends[k, j] = gate_up(me ^ (k * minor + j)).astype(bf16)
    both = lambda x, lo, hi: jnp.concatenate([x[:, lo:hi], x[:, block + lo : block + hi]], axis=1)
    for i, (lo, hi) in enumerate(subs):
        for k in turns:
            arrived[i, k] = [swap(both(sends[k, j], lo, hi), "gy", j) for j in range(1, minor)]
    own = {k: lax.optimization_barrier(gate_up(me ^ (k * minor))) for k in turns}
    mark = me - major * len(subs)
    for _ in range(major * len(subs)):
        mark = lax.optimization_barrier(mark + 1)
    down = 0.0
    for i, (lo, hi) in enumerate(subs):
        for k in turns:
            total = both(own[k], lo, hi)
            for part in arrived[i, k]:
                total = total + part.astype(f32)
            if k:
                bit = k & -k
                arrived[i, k ^ bit].append(swap(total.astype(bf16), "gy", bit * minor))
        total = total * factor[:, None]
        activation = (jax.nn.silu(total[:, : hi - lo]) * total[:, hi - lo :]).astype(bf16)
        for index, part in gather_blocks(activation, "gy", mark):
            down = down + mm(part, lax.dynamic_slice_in_dim(w_down, index * block + lo, hi - lo, 0))
    after_mlp = add_over(down, after_attention, "gx")

    tokens = scaled(after_mlp, final_gain)
    factor = factor_of(after_mlp, width)
    own_factor = pick(factor.reshape(gy, local), me)
    vocab = w_head.shape[1]
    starts = head_starts(vocab)
    first = lax.axis_index("gx") * vocab
    target = lax.optimization_barrier(draft_ids - first)
    pieces, targets = [], []
    for c, (start, stop) in enumerate(zip(starts[:-1], starts[1:], strict=True)):
        if c:
            target = lax.optimization_barrier(target - (start - starts[c - 1]))
        targets.append(target)
        logits = mm(tokens, w_head[:, start:stop])
        pieces.append(scatter_rows(logits, "gy") * own_factor[:, None])
    tops, sums, picked = [], [], 0.0
    for target, piece in zip(targets, pieces, strict=True):
        ids = jnp.arange(piece.shape[1], dtype=jnp.int32)[None, :]
        picked = picked + jnp.sum(jnp.where(ids == target[:, None], piece, 0.0), axis=1)
        top = jnp.max(piece, axis=1)
        tops.append(top)
        sums.append(jnp.sum(jnp.exp(piece - top[:, None]), axis=1))
    top = jnp.max(jnp.stack(tops), axis=0)
    total = sum(s * jnp.exp(t - top) for s, t in zip(sums, tops, strict=True))
    stats = jnp.stack([top, total, picked])
    mask = 1
    while mask < lax.axis_size("gx"):
        other = swap(stats, "gx", mask)
        high = jnp.maximum(stats[0], other[0])
        stats = jnp.stack(
            [
                high,
                stats[1] * jnp.exp(stats[0] - high) + other[1] * jnp.exp(other[0] - high),
                stats[2] + other[2],
            ]
        )
        mask *= 2
    normalizer = stats[0] + jnp.log(stats[1])
    return (jnp.concatenate(pieces, axis=1) - normalizer[:, None], stats[2] - normalizer)


def cuts(block):
    middle = max(1, round(block * 0.55 / 128)) * 128
    return [(0, middle), (middle, block)] if middle < block else [(0, block)]


def visits(major):
    return sorted(range(major), key=lambda k: (k & -k or major, -k))


def solution(mesh):
    return jax.shard_map(
        shards,
        mesh=mesh,
        in_specs=(
            P("gx", "gy"), P("gy"), P("gy"), P("gy"), P("gy", "gx"), P("gy", "gx"), P("gy", "gx"),
            P("gx", "gy"), P("gy", "gx", None, None), P("gy", "gx", None, None), P("gy"),
            P("gy", "gx"), P("gy", "gx"), P("gx", "gy"), P("gy"), P("gy", "gx"),
        ),
        out_specs=(P("gy", "gx"), P("gy")),
        check_vma=False,
    )
```
